512 devices in a mesh: tm: 16 (over z_hi, y, core), seq: 32 (over x, z_lo).
Axes of the slice: x: 4, y: 4, z: 16 (z_hi: 2, z_lo: 8; z = z_hi * 8 + z_lo), core: 2. Of those that a mesh axis runs over, the one named last changes fastest.
Arguments:
- queries: bfloat16 [16, 768, 4096], P('tm', 'seq'), may hold values from -144 to 144
- keys_proj: bfloat16 [16, 768, 4096], P('tm', 'seq'), may hold values from -12 to 12
- values: bfloat16 [16, 768, 4096], P('tm', 'seq'), may hold values from -4 to 4
- hidden: bfloat16 [16, 768, 4096], P('tm', 'seq'), may hold values from -4 to 4
- fresh_latent: bfloat16 [768, 4096], P('seq'), may hold values from -4 to 4
- gate_table: float32 [50, 4096], replicated, may hold values from 0.5 to 2.5
- noise_step: int32 [16], P('tm'), may hold values from 0 to 49, as said below
- pattern: int32 [16, 16], replicated, may hold values from 0 to 1, as said below
Outputs:
- advanced: bfloat16 [16, 768, 4096], P('tm', 'seq')
- next_cache: bfloat16 [16, 2, 768, 4096], P('tm', None, None, 'seq')
The draws below stay inside these ranges and needn't reach their ends.
Inputs may be any that keep to these rules, and one draw needn't show every extreme that they name: pattern[i][0] is 1 for every i, and pattern[i][j] is 0 where j > i. noise_step[0] is 0, noise_step[15] is 49, and all 16 values are distinct.
All inputs are finite; a program needn't handle non-finite values.
Results may differ from the reference program's by a relative error of at most 0.0036.
Values may be sent and summed in bfloat16 or wider, within the bound.
A program may use at most 64 MiB of HBM per device.

```python
import math
import jax
import jax.numpy as jnp
from jax import lax

HD = 128
HEADS = 32
STEPS = 50
WID = 4096
GROUPS = 16
GROUP_TOK = 768


def paired_draw(key):
    base_keys = jnp.clip(jax.random.normal(jax.random.fold_in(key, 101), (GROUPS, GROUP_TOK, WID), jnp.float32), -4.0, 4.0)
    base_queries = 2.0 * jnp.clip(jax.random.normal(jax.random.fold_in(key, 202), (GROUPS, GROUP_TOK, WID), jnp.float32), -4.0, 4.0)
    keys_out = base_keys
    queries_out = base_queries
    return (queries_out, keys_out)


def draw_queries(key, part):
    return paired_draw(key)[0].astype(jnp.bfloat16)


def draw_keys_proj(key, part):
    return paired_draw(key)[1].astype(jnp.bfloat16)


def draw_pattern(key, part):
    coins = jax.random.randint(jax.random.fold_in(key, 404), (GROUPS, GROUPS), 0, 2, jnp.int32)
    row_index = jnp.arange(GROUPS, dtype=jnp.int32)[:, None]
    col_index = jnp.arange(GROUPS, dtype=jnp.int32)[None, :]
    return jnp.where(col_index == 0, 1, jnp.where(col_index <= row_index, coins, 0)).astype(jnp.int32)


def draw_noise_step(key, part):
    middle = 1 + jax.random.permutation(jax.random.fold_in(key, 505), STEPS - 2)[:GROUPS - 2].astype(jnp.int32)
    first = jnp.zeros((1,), jnp.int32)
    final = jnp.full((1,), STEPS - 1, jnp.int32)
    return jnp.concatenate([first, middle, final], axis=0).astype(jnp.int32)


def steps_of(rng, shape, shards, least, largest):
    def one(position, shards_of):
        steps = jax.random.uniform(jax.random.fold_in(jax.random.fold_in(rng, 6), position), (shards_of,), jnp.float32, least / len(shards), largest / len(shards))
        return jnp.repeat(jnp.exp(steps), shape[position] // shards_of).reshape((-1,) + (1,) * (len(shape) - position - 1))

    loudness = one(*shards[0])
    for cut in shards[1:]:
        loudness = loudness * one(*cut)
    return loudness


def noise(key, dims, deviation, most, shards=(), kind=jnp.bfloat16):
    array = deviation * jax.random.normal(key, dims, jnp.float32)
    if shards:
        array = array * steps_of(key, dims, shards, -0.22, 0.18)
    return jnp.clip(array, -most, most).astype(kind)


def setup_inputs(seed: int = 0) -> dict:
    splits = jax.random.split(jax.random.key(seed), 9)
    return {
        "queries": draw_queries(jax.random.fold_in(splits[8], 71), 0),
        "keys_proj": draw_keys_proj(jax.random.fold_in(splits[8], 71), 0),
        "values": noise(splits[2], (GROUPS, GROUP_TOK, WID), 1.0, 4.0, ((0, 16), (1, 32))),
        "hidden": noise(splits[3], (GROUPS, GROUP_TOK, WID), 1.0, 4.0, ((0, 16), (1, 32))),
        "fresh_latent": noise(splits[4], (GROUP_TOK, WID), 1.0, 4.0, ((0, 32),)),
        "gate_table": jnp.clip(jax.random.uniform(splits[5], (STEPS, WID), jnp.float32, 0.5, 2.5), 0.5, 2.5),
        "noise_step": draw_noise_step(jax.random.fold_in(splits[8], 71), 0),
        "pattern": draw_pattern(jax.random.fold_in(splits[8], 71), 0),
    }


def group_attention(query_group, reach_row, key_heads, value_heads):
    query_heads = jnp.transpose(query_group.reshape(GROUP_TOK, HEADS, HD), (1, 0, 2))
    live = jnp.repeat(reach_row, GROUP_TOK) > 0
    scale_factor = 1.0 / math.sqrt(HD)

    def one_head(inputs):
        query_one, key_one, value_one = inputs
        scores = jnp.dot(query_one, key_one.T, preferred_element_type=jnp.float32) * scale_factor
        scores = jnp.where(live[None, :], scores, jnp.float32(-1e+30))
        highest = lax.optimization_barrier(jnp.max(scores, axis=-1, keepdims=True))
        raised = jnp.exp(scores - highest)
        total = lax.optimization_barrier(jnp.sum(raised, axis=-1))
        probs = raised.astype(jnp.bfloat16)
        numer = jnp.dot(probs, value_one, preferred_element_type=jnp.float32)
        return numer / total[:, None]
    result = lax.map(one_head, (query_heads, key_heads, value_heads))
    return jnp.transpose(result, (1, 0, 2)).reshape(GROUP_TOK, WID).astype(jnp.bfloat16)

def reference(queries, keys_proj, values, hidden, fresh_latent, gate_table, noise_step, pattern):
    key_heads = jnp.transpose(keys_proj.reshape(GROUPS * GROUP_TOK, HEADS, HD), (1, 0, 2))
    value_heads = jnp.transpose(values.reshape(GROUPS * GROUP_TOK, HEADS, HD), (1, 0, 2))

    def per_group(inputs):
        query_group, reach_row = inputs
        return group_attention(query_group, reach_row, key_heads, value_heads)
    attended = lax.map(per_group, (queries, pattern))
    gates = gate_table[noise_step]
    updated = (hidden.astype(jnp.float32) + gates[:, None, :] * attended.astype(jnp.float32)).astype(jnp.bfloat16)
    advanced = jnp.concatenate([updated[1:], fresh_latent[None]], axis=0)
    blank = jnp.zeros((1, GROUP_TOK, WID), keys_proj.dtype)
    next_keys = jnp.concatenate([keys_proj[1:], blank], axis=0)
    next_values = jnp.concatenate([values[1:], blank], axis=0)
    next_cache = jnp.stack([next_keys, next_values], axis=1)
    return (advanced, next_cache)
```

```python
import functools
import math

import jax
import jax.numpy as jnp
from jax import lax
from jax.experimental import pallas as pl
from jax.experimental.pallas import tpu as pltpu
from jax.sharding import PartitionSpec as P

HD = 128
NG = 16
NS = 32
TOK = 24
ROWS = 768
MESH = pl.DeviceIdType.MESH
LOG2E = math.log2(math.e)


def remote(src, dst, send_sem, recv_sem, g, s):
    return pltpu.make_async_remote_copy(
        src_ref=src,
        dst_ref=dst,
        send_sem=send_sem,
        recv_sem=recv_sem,
        device_id=(g, s),
        device_id_type=MESH,
    )


def drain(ref, sem):
    pltpu.make_async_copy(ref, ref, sem).wait()


def signal(sem, g, s):
    pl.semaphore_signal(sem, inc=1, device_id=(g, s), device_id_type=MESH)


def exchange_kernel(
    k_ref,
    v_ref,
    q_ref,
    hid_ref,
    gate_ref,
    kv_ref,
    qh_ref,
    hid_next_ref,
    gate_next_ref,
    p1_send,
    p1_recv,
    q_send,
    q_recv,
    ring_send,
    ring_recv,
    relay_send,
    relay_recv,
    sib_send,
    sib_recv,
    hid_send,
    hid_recv,
):
    g = lax.axis_index("tm")
    s = lax.axis_index("seq")
    z = g // 8
    y = (g % 8) // 2
    c = g % 2
    right = (y + 1) % 4
    left = (y + 3) % 4
    across = (y + 2) % 4
    partner = (g + 8) % 16
    g_right = 8 * z + 2 * right + c
    g_left = 8 * z + 2 * left + c
    g_sib = 8 * z + 2 * y + 1 - c

    barrier = pltpu.get_barrier_semaphore()

    def greet_seq(i, carry):
        signal(barrier, g, (s + i) % NS)
        return carry

    def greet_partner(i, carry):
        signal(barrier, partner, (s + i) % NS)
        return carry

    lax.fori_loop(1, NS, greet_seq, 0)
    lax.fori_loop(0, NS, greet_partner, 0)
    signal(barrier, g_right, s)
    signal(barrier, g_left, s)
    signal(barrier, g_sib, s)

    @pl.when(g == 7)
    def _():
        lax.fori_loop(0, NS, lambda i, x: (signal(barrier, 8, (s + i) % NS), x)[1], 0)

    @pl.when(g == 8)
    def _():
        lax.fori_loop(0, NS, lambda i, x: (signal(barrier, 7, (s + i) % NS), x)[1], 0)

    @pl.when((c == 1) & (g < 15) & (g != 7))
    def _():
        signal(barrier, g + 1, s)

    @pl.when((c == 0) & (g > 0) & (g != 8))
    def _():
        signal(barrier, g - 1, s)

    extra = jnp.where(
        (g == 7) | (g == 8),
        NS,
        jnp.where((g == 0) | (g == 15), 0, 1),
    )
    pl.semaphore_wait(barrier, NS - 1 + NS + 3 + extra)

    row = pl.multiple_of(s * TOK, 8)

    def near(src, dst, send_sem, recv_sem, h):
        cols = pl.ds(pl.multiple_of(h * HD, HD), HD)
        remote(src.at[:, cols], dst.at[pl.ds(row, TOK)], send_sem, recv_sem, g, h).start()

    for kind, src in ((0, k_ref), (1, v_ref)):
        own = pl.ds(pl.multiple_of(s * HD, HD), HD)
        pltpu.make_async_copy(
            src.at[:, own], kv_ref.at[g, kind, pl.ds(row, TOK)], p1_recv.at[0, kind]
        ).start()

        def send_low(i, carry, kind=kind, src=src):
            h = (s + i) % NS
            cols = pl.ds(pl.multiple_of(h * HD, HD), HD)
            remote(
                src.at[:, cols],
                kv_ref.at[g, kind, pl.ds(row, TOK)],
                p1_send.at[1, kind],
                p1_recv.at[1, kind],
                g + 8,
                h,
            ).start()
            return carry

        def send_near(i, carry, kind=kind, src=src):
            h = (s + i) % NS
            near(src, kv_ref.at[g, kind], p1_send.at[0, kind], p1_recv.at[0, kind], h)
            return carry

        def send_down(i, carry, kind=kind, src=src):
            h = (s + i) % NS
            cols = pl.ds(pl.multiple_of(h * HD, HD), HD)
            remote(
                src.at[:, cols],
                kv_ref.at[8, kind, pl.ds(row, TOK)],
                p1_send.at[1, kind],
                p1_recv.at[1, kind],
                7,
                h,
            ).start()
            return carry

        @pl.when(z == 0)
        def _(send_low=send_low):
            lax.fori_loop(0, NS, send_low, 0)

        lax.fori_loop(1, NS, send_near, 0)

        @pl.when(g == 8)
        def _(send_down=send_down):
            lax.fori_loop(0, NS, send_down, 0)

    own = pl.ds(pl.multiple_of(s * HD, HD), HD)
    pltpu.make_async_copy(q_ref.at[:, own], qh_ref.at[pl.ds(row, TOK)], q_recv).start()

    def send_q(i, carry):
        near(q_ref, qh_ref, q_send, q_recv, (s + i) % NS)
        return carry

    lax.fori_loop(1, NS, send_q, 0)

    @pl.when(g > 0)
    def _():
        remote(hid_ref, hid_next_ref, hid_send.at[0], hid_recv.at[0], g - 1, s).start()
        remote(gate_ref, gate_next_ref, hid_send.at[1], hid_recv.at[1], g - 1, s).start()

    def slot(ab, yy, cc):
        return 8 * z * (1 - ab) + 2 * yy + cc

    def ring(kind, ab, way, target):
        piece = kv_ref.at[slot(ab, y, c), kind]
        return remote(piece, piece, ring_send.at[kind, ab, way], ring_recv.at[kind, ab, way], target, s)

    def relay(kind, ab):
        owner = left if kind == 0 else right
        target = g_right if kind == 0 else g_left
        piece = kv_ref.at[slot(ab, owner, c), kind]
        return remote(piece, piece, relay_send.at[kind, ab], relay_recv.at[kind, ab], target, s)

    def sib(kind, ab, yy):
        piece = kv_ref.at[slot(ab, yy, c), kind]
        return remote(piece, piece, sib_send.at[kind, ab, yy], sib_recv.at[kind, ab, yy], g_sib, s)

    for kind in (0, 1):

        def open_own(ab, carry, kind=kind):
            drain(kv_ref.at[slot(ab, y, c), kind], p1_recv.at[ab, kind])
            ring(kind, ab, 0, g_right).start()
            ring(kind, ab, 1, g_left).start()
            sib(kind, ab, y).start()
            return carry

        def open_ring(ab, carry, kind=kind):
            drain(kv_ref.at[slot(ab, left, c), kind], ring_recv.at[kind, ab, 0])
            if kind == 0:
                relay(kind, ab).start()
            sib(kind, ab, left).start()
            drain(kv_ref.at[slot(ab, right, c), kind], ring_recv.at[kind, ab, 1])
            if kind == 1:
                relay(kind, ab).start()
            sib(kind, ab, right).start()
            return carry

        def open_across(ab, carry, kind=kind):
            drain(kv_ref.at[slot(ab, across, c), kind], relay_recv.at[kind, ab])
            sib(kind, ab, across).start()
            return carry

        lax.fori_loop(0, z + 1, open_own, 0)
        lax.fori_loop(0, z + 1, open_ring, 0)
        lax.fori_loop(0, z + 1, open_across, 0)

    for kind in (0, 1):

        @pl.when(g == 7)
        def _(kind=kind):
            drain(kv_ref.at[8, kind], p1_recv.at[1, kind])

        def close(ab, carry, kind=kind):
            def close_sib(yy, inner):
                drain(kv_ref.at[slot(ab, yy, 1 - c), kind], sib_recv.at[kind, ab, yy])
                sib(kind, ab, yy).wait_send()
                return inner

            lax.fori_loop(0, 4, close_sib, 0)
            ring(kind, ab, 0, g_right).wait_send()
            ring(kind, ab, 1, g_left).wait_send()
            relay(kind, ab).wait_send()
            return carry

        lax.fori_loop(0, z + 1, close, 0)
        drain(kv_ref.at[g, kind, pl.ds(0, ROWS - TOK)], p1_send.at[0, kind])

        @pl.when((z == 0) | (g == 8))
        def _(kind=kind):
            drain(kv_ref.at[g, kind], p1_send.at[1, kind])

    drain(qh_ref, q_recv)
    drain(qh_ref.at[pl.ds(0, ROWS - TOK)], q_send)

    @pl.when(g > 0)
    def _():
        remote(hid_ref, hid_next_ref, hid_send.at[0], hid_recv.at[0], g - 1, s).wait_send()
        remote(gate_ref, gate_next_ref, hid_send.at[1], hid_recv.at[1], g - 1, s).wait_send()

    @pl.when(g < 15)
    def _():
        drain(hid_next_ref, hid_recv.at[0])
        drain(gate_next_ref, hid_recv.at[1])


def exchange(keys, values, queries, hidden, gate_row):
    vmem = pl.BlockSpec(memory_space=pltpu.VMEM)
    hbm = pl.BlockSpec(memory_space=pl.ANY)
    dma = pltpu.SemaphoreType.DMA
    return pl.pallas_call(
        exchange_kernel,
        out_shape=(
            jax.ShapeDtypeStruct((NG, 2, ROWS, HD), jnp.bfloat16),
            jax.ShapeDtypeStruct((ROWS, HD), jnp.bfloat16),
            jax.ShapeDtypeStruct(hidden.shape, jnp.bfloat16),
            jax.ShapeDtypeStruct(gate_row.shape, jnp.float32),
        ),
        in_specs=[vmem] * 5,
        out_specs=(hbm,) * 4,
        scratch_shapes=[
            dma((2, 2)),
            dma((2, 2)),
            dma,
            dma,
            dma((2, 2, 2)),
            dma((2, 2, 2)),
            dma((2, 2)),
            dma((2, 2)),
            dma((2, 2, 4)),
            dma((2, 2, 4)),
            dma((2,)),
            dma((2,)),
        ],
        compiler_params=pltpu.CompilerParams(collective_id=0, has_side_effects=True),
        name="exchange",
    )(keys, values, queries, hidden, gate_row)


def attend_kernel(pattern_ref, group_ref, q_ref, kv_ref, next_ref, o_ref, cache_ref, acc, high, total):
    j = pl.program_id(0)
    g = group_ref[0]

    @pl.when(j == 0)
    def _():
        acc[...] = jnp.zeros_like(acc)
        total[...] = jnp.zeros_like(total)
        high[...] = jnp.full_like(high, -1e30)
        cache_ref[...] = jnp.where(g < NG - 1, next_ref[0], jnp.zeros_like(cache_ref))

    @pl.when((j <= g) & (pattern_ref[g, j] > 0))
    def _():
        keys = kv_ref[0, 0]
        values_t = kv_ref[0, 1].T
        width = 256
        for at in range(0, ROWS, width):
            span = pl.ds(at, width)
            scores = lax.dot_general(
                keys, q_ref[span, :], (((1,), (1,)), ((), ())), preferred_element_type=jnp.float32
            ) * (LOG2E / math.sqrt(HD))
            before = high[:, span]
            raised = jnp.maximum(before, jnp.max(scores, axis=0, keepdims=True))
            fade = jnp.exp2(before - raised)
            probs = jnp.exp2(scores - raised)
            high[:, span] = raised
            total[:, span] = total[:, span] * fade + jnp.sum(probs, axis=0, keepdims=True)
            acc[:, span] = acc[:, span] * fade + jnp.dot(
                values_t, probs.astype(jnp.bfloat16), preferred_element_type=jnp.float32
            )

    @pl.when(j == NG - 1)
    def _():
        o_ref[...] = (acc[...] / total[...]).T.astype(jnp.bfloat16)


def attend(pattern, group, qh, kv):
    grid_spec = pltpu.PrefetchScalarGridSpec(
        num_scalar_prefetch=2,
        grid=(NG,),
        in_specs=[
            pl.BlockSpec((ROWS, HD), lambda j, p, g: (0, 0)),
            pl.BlockSpec((1, 2, ROWS, HD), lambda j, p, g: (jnp.minimum(j, g[0]), 0, 0, 0)),
            pl.BlockSpec((1, 2, ROWS, HD), lambda j, p, g: (jnp.minimum(g[0] + 1, NG - 1), 0, 0, 0)),
        ],
        out_specs=[
            pl.BlockSpec((ROWS, HD), lambda j, p, g: (0, 0)),
            pl.BlockSpec((2, ROWS, HD), lambda j, p, g: (0, 0, 0)),
        ],
        scratch_shapes=[
            pltpu.VMEM((HD, ROWS), jnp.float32),
            pltpu.VMEM((1, ROWS), jnp.float32),
            pltpu.VMEM((1, ROWS), jnp.float32),
        ],
    )
    return pl.pallas_call(
        attend_kernel,
        out_shape=(
            jax.ShapeDtypeStruct((ROWS, HD), jnp.bfloat16),
            jax.ShapeDtypeStruct((2, ROWS, HD), jnp.bfloat16),
        ),
        grid_spec=grid_spec,
        name="attend",
    )(pattern, group, qh, kv, kv)


def return_kernel(o_ref, hid_ref, gate_ref, fresh_ref, out_ref, landed, send_sem, recv_sem):
    g = lax.axis_index("tm")
    s = lax.axis_index("seq")
    barrier = pltpu.get_barrier_semaphore()

    @pl.when(g > 0)
    def _():
        lax.fori_loop(0, NS, lambda i, x: (signal(barrier, g - 1, (s + i) % NS), x)[1], 0)

    @pl.when(g < NG - 1)
    def _():
        lax.fori_loop(0, NS, lambda i, x: (signal(barrier, g + 1, (s + i) % NS), x)[1], 0)

    pl.semaphore_wait(barrier, jnp.where((g == 0) | (g == NG - 1), NS, 2 * NS))
    cols = pl.ds(pl.multiple_of(s * HD, HD), HD)

    @pl.when(g > 0)
    def _():
        def send(i, carry):
            t = (s + i) % NS
            remote(
                o_ref.at[pl.ds(pl.multiple_of(t * TOK, 8), TOK)],
                landed.at[:, cols],
                send_sem,
                recv_sem,
                g - 1,
                t,
            ).start()
            return carry

        lax.fori_loop(0, NS, send, 0)
        drain(o_ref, send_sem)

    @pl.when(g < NG - 1)
    def _():
        drain(landed, recv_sem)
        out_ref[...] = (
            hid_ref[...].astype(jnp.float32) + gate_ref[...] * landed[...].astype(jnp.float32)
        ).astype(jnp.bfloat16)

    @pl.when(g == NG - 1)
    def _():
        out_ref[...] = fresh_ref[...]


def give_back(o, hid_next, gate_next, fresh):
    vmem = pl.BlockSpec(memory_space=pltpu.VMEM)
    dma = pltpu.SemaphoreType.DMA
    return pl.pallas_call(
        return_kernel,
        out_shape=jax.ShapeDtypeStruct(fresh.shape, jnp.bfloat16),
        in_specs=[vmem] * 4,
        out_specs=vmem,
        scratch_shapes=[pltpu.VMEM(fresh.shape, jnp.bfloat16), dma, dma],
        compiler_params=pltpu.CompilerParams(collective_id=1, has_side_effects=True),
        name="give_back",
    )(o, hid_next, gate_next, fresh)


def body(queries, keys_proj, values, hidden, fresh_latent, gate_table, noise_step, pattern):
    group = lax.axis_index("tm").astype(jnp.int32).reshape(1)
    gate_row = lax.dynamic_slice_in_dim(gate_table, noise_step[0], 1, 0)
    kv, qh, hid_next, gate_next = exchange(keys_proj[0], values[0], queries[0], hidden[0], gate_row)
    attended, next_cache = attend(pattern, group, qh, kv)
    advanced = give_back(attended, hid_next, gate_next, fresh_latent)
    return (advanced[None], next_cache[None])


def solution(mesh):
    placed = (
        P("tm", "seq", None),
        P("tm", "seq", None),
        P("tm", "seq", None),
        P("tm", "seq", None),
        P("seq", None),
        P(),
        P("tm"),
        P(),
    )
    return jax.shard_map(
        body,
        mesh=mesh,
        in_specs=placed,
        out_specs=(P("tm", "seq", None), P("tm", None, None, "seq")),
        check_vma=False,
    )
```

```python
import functools
import math

import jax
import jax.numpy as jnp
from jax import lax
from jax.experimental import pallas as pl
from jax.experimental.pallas import tpu as pltpu
from jax.sharding import PartitionSpec as P

HD = 128
NG = 16
NS = 32
TOK = 24
ROWS = 768
MESH = pl.DeviceIdType.MESH
LOG2E = math.log2(math.e)


def remote(src, dst, send_sem, recv_sem, g, s):
    return pltpu.make_async_remote_copy(
        src_ref=src,
        dst_ref=dst,
        send_sem=send_sem,
        recv_sem=recv_sem,
        device_id=(g, s),
        device_id_type=MESH,
    )


def drain(ref, sem):
    pltpu.make_async_copy(ref, ref, sem).wait()


def signal(sem, g, s):
    pl.semaphore_signal(sem, inc=1, device_id=(g, s), device_id_type=MESH)


def exchange_kernel(
    k_ref,
    v_ref,
    q_ref,
    hid_ref,
    gate_ref,
    kv_ref,
    qh_ref,
    cache_ref,
    hid_next_ref,
    gate_next_ref,
    p1_send,
    p1_recv,
    q_send,
    q_recv,
    pair_send,
    pair_recv,
    ring_send,
    ring_recv,
    relay_send,
    relay_recv,
    sib_send,
    sib_recv,
    cache_send,
    cache_recv,
    hid_send,
    hid_recv,
):
    g = lax.axis_index("tm")
    s = lax.axis_index("seq")
    z = g // 8
    y = (g % 8) // 2
    c = g % 2
    x = s // 8
    zl = s % 8
    p = x % 2
    role = 8 * p + 2 * y + c
    head = 8 * (x - p + z) + zl
    right = (y + 1) % 4
    left = (y + 3) % 4
    across = (y + 2) % 4
    g_right = 8 * z + 2 * right + c
    g_left = 8 * z + 2 * left + c
    g_sib = 8 * z + 2 * y + 1 - c
    s_pair = s + 8 - 16 * p
    own = jnp.where(p == z, 1, 0)
    far_cache = (g < 15) & ((p != z) | (g == 7))

    barrier = pltpu.get_barrier_semaphore()

    def greet(tm, start):
        def step(i, carry):
            signal(barrier, tm, (s + i) % NS)
            return carry

        lax.fori_loop(start, NS, step, 0)

    greet(role, own)
    signal(barrier, g_right, s)
    signal(barrier, g_left, s)
    signal(barrier, g_sib, s)

    @pl.when(p == 1)
    def _():
        signal(barrier, g, s_pair)

    @pl.when(g < 15)
    def _():
        signal(barrier, g + 1, s)

    @pl.when(far_cache)
    def _():
        greet(g + 1, 0)

    pl.semaphore_wait(
        barrier,
        NS - own + 3 + (1 - p) + jnp.where(g > 0, 1 + NS // 2, 0) + jnp.where(g == 8, NS // 2, 0),
    )

    row = pl.ds(pl.multiple_of(s * TOK, 8), TOK)

    def columns(h):
        return pl.ds(pl.multiple_of(h * HD, HD), HD)

    def scatter(src, dst, send_sem, recv_sem):
        @pl.when(own == 1)
        def _():
            pltpu.make_async_copy(src.at[:, columns(head)], dst.at[row], recv_sem).start()

        def step(i, carry):
            h = (head + i) % NS
            xh = h // 8
            tm = 8 * (xh % 2) + 2 * y + c
            seq = 8 * (xh - xh % 2 + z) + h % 8
            remote(src.at[:, columns(h)], dst.at[row], send_sem, recv_sem, tm, seq).start()
            return carry

        lax.fori_loop(own, NS, step, 0)

    def scattered(dst, send_sem):
        @pl.when(own == 1)
        def _():
            drain(dst.at[pl.ds(0, ROWS - TOK)], send_sem)

        @pl.when(own == 0)
        def _():
            drain(dst, send_sem)

    scatter(k_ref, kv_ref.at[g, 0], p1_send.at[0], p1_recv.at[0])
    scatter(v_ref, kv_ref.at[g, 1], p1_send.at[1], p1_recv.at[1])
    scatter(q_ref, qh_ref, q_send, q_recv)

    @pl.when(g > 0)
    def _():
        remote(hid_ref, hid_next_ref, hid_send.at[0], hid_recv.at[0], g - 1, s).start()
        remote(gate_ref, gate_next_ref, hid_send.at[1], hid_recv.at[1], g - 1, s).start()

    below = (g - 1) // 8
    for kind, src in ((0, k_ref), (1, v_ref)):

        def cache_step(i, carry, kind=kind, src=src, flip=1):
            j = (s + i) % (NS // 2)
            h = 16 * (j // 8) + 8 * (flip + below - 2 * flip * below) + j % 8
            remote(
                src.at[:, columns(h)],
                cache_ref.at[kind, row],
                cache_send.at[kind],
                cache_recv.at[kind],
                g - 1,
                h,
            ).start()
            return carry

        @pl.when(g > 0)
        def _(cache_step=cache_step):
            lax.fori_loop(0, NS // 2, cache_step, 0)

        @pl.when(g == 8)
        def _(cache_step=cache_step):
            lax.fori_loop(0, NS // 2, functools.partial(cache_step, flip=0), 0)

    def slot(ab, yy, cc):
        return 8 * p * (1 - ab) + 2 * yy + cc

    def pair(kind):
        piece = kv_ref.at[2 * y + c, kind]
        return remote(piece, piece, pair_send.at[kind], pair_recv.at[kind], g, s_pair)

    def ring(kind, ab, way, target):
        piece = kv_ref.at[slot(ab, y, c), kind]
        return remote(piece, piece, ring_send.at[kind, ab, way], ring_recv.at[kind, ab, way], target, s)

    def relay(kind, ab):
        owner = left if kind == 0 else right
        target = g_right if kind == 0 else g_left
        piece = kv_ref.at[slot(ab, owner, c), kind]
        return remote(piece, piece, relay_send.at[kind, ab], relay_recv.at[kind, ab], target, s)

    def sib(kind, ab, yy):
        piece = kv_ref.at[slot(ab, yy, c), kind]
        return remote(piece, piece, sib_send.at[kind, ab, yy], sib_recv.at[kind, ab, yy], g_sib, s)

    for kind in (0, 1):

        def open_own(ab, carry, kind=kind):
            @pl.when(ab == 0)
            def _():
                drain(kv_ref.at[slot(ab, y, c), kind], p1_recv.at[kind])

                @pl.when(p == 0)
                def _():
                    pair(kind).start()

            @pl.when(ab == 1)
            def _():
                drain(kv_ref.at[slot(ab, y, c), kind], pair_recv.at[kind])

            ring(kind, ab, 0, g_right).start()
            ring(kind, ab, 1, g_left).start()
            sib(kind, ab, y).start()
            return carry

        def open_ring(ab, carry, kind=kind):
            drain(kv_ref.at[slot(ab, left, c), kind], ring_recv.at[kind, ab, 0])
            if kind == 0:
                relay(kind, ab).start()
            sib(kind, ab, left).start()
            drain(kv_ref.at[slot(ab, right, c), kind], ring_recv.at[kind, ab, 1])
            if kind == 1:
                relay(kind, ab).start()
            sib(kind, ab, right).start()
            return carry

        def open_across(ab, carry, kind=kind):
            drain(kv_ref.at[slot(ab, across, c), kind], relay_recv.at[kind, ab])
            sib(kind, ab, across).start()
            return carry

        lax.fori_loop(0, p + 1, open_own, 0)
        lax.fori_loop(0, p + 1, open_ring, 0)
        lax.fori_loop(0, p + 1, open_across, 0)

    for kind in (0, 1):

        def close(ab, carry, kind=kind):
            def close_sib(yy, inner):
                drain(kv_ref.at[slot(ab, yy, 1 - c), kind], sib_recv.at[kind, ab, yy])
                sib(kind, ab, yy).wait_send()
                return inner

            lax.fori_loop(0, 4, close_sib, 0)
            ring(kind, ab, 0, g_right).wait_send()
            ring(kind, ab, 1, g_left).wait_send()
            relay(kind, ab).wait_send()
            return carry

        lax.fori_loop(0, p + 1, close, 0)
        scattered(kv_ref.at[role, kind], p1_send.at[kind])

        @pl.when(p == 0)
        def _(kind=kind):
            pair(kind).wait_send()

        @pl.when(far_cache)
        def _(kind=kind):
            drain(cache_ref.at[kind], cache_recv.at[kind])

        @pl.when(g > 0)
        def _(kind=kind):
            drain(cache_ref.at[kind, pl.ds(0, ROWS // 2)], cache_send.at[kind])

        @pl.when(g == 8)
        def _(kind=kind):
            drain(cache_ref.at[kind, pl.ds(0, ROWS // 2)], cache_send.at[kind])

    drain(qh_ref, q_recv)
    scattered(qh_ref, q_send)

    @pl.when(g > 0)
    def _():
        remote(hid_ref, hid_next_ref, hid_send.at[0], hid_recv.at[0], g - 1, s).wait_send()
        remote(gate_ref, gate_next_ref, hid_send.at[1], hid_recv.at[1], g - 1, s).wait_send()

    @pl.when(g < 15)
    def _():
        drain(hid_next_ref, hid_recv.at[0])
        drain(gate_next_ref, hid_recv.at[1])


def exchange(keys, values, queries, hidden, gate_row):
    vmem = pl.BlockSpec(memory_space=pltpu.VMEM)
    hbm = pl.BlockSpec(memory_space=pl.ANY)
    dma = pltpu.SemaphoreType.DMA
    return pl.pallas_call(
        exchange_kernel,
        out_shape=(
            jax.ShapeDtypeStruct((NG, 2, ROWS, HD), jnp.bfloat16),
            jax.ShapeDtypeStruct((ROWS, HD), jnp.bfloat16),
            jax.ShapeDtypeStruct((2, ROWS, HD), jnp.bfloat16),
            jax.ShapeDtypeStruct(hidden.shape, jnp.bfloat16),
            jax.ShapeDtypeStruct(gate_row.shape, jnp.float32),
        ),
        in_specs=[vmem] * 5,
        out_specs=(hbm,) * 5,
        scratch_shapes=[
            dma((2,)),
            dma((2,)),
            dma,
            dma,
            dma((2,)),
            dma((2,)),
            dma((2, 2, 2)),
            dma((2, 2, 2)),
            dma((2, 2)),
            dma((2, 2)),
            dma((2, 2, 4)),
            dma((2, 2, 4)),
            dma((2,)),
            dma((2,)),
            dma((2,)),
            dma((2,)),
        ],
        compiler_params=pltpu.CompilerParams(collective_id=0, has_side_effects=True),
        name="exchange",
    )(keys, values, queries, hidden, gate_row)


def attend_kernel(
    pattern_ref, place_ref, q_ref, kv_ref, next_ref, far_ref, o_ref, cache_ref, acc, high, total
):
    j = pl.program_id(0)
    g = place_ref[0]

    @pl.when(j == 0)
    def _():
        acc[...] = jnp.zeros_like(acc)
        total[...] = jnp.zeros_like(total)
        high[...] = jnp.full_like(high, -1e30)
        near = jnp.where(place_ref[2] > 0, far_ref[...], next_ref[0])
        cache_ref[...] = jnp.where(place_ref[1] < NG - 1, near, jnp.zeros_like(near))

    @pl.when((j <= g) & (pattern_ref[g, j] > 0))
    def _():
        keys = kv_ref[0, 0]
        values_t = kv_ref[0, 1].T
        width = 256
        for at in range(0, ROWS, width):
            span = pl.ds(at, width)
            scores = lax.dot_general(
                keys, q_ref[span, :], (((1,), (1,)), ((), ())), preferred_element_type=jnp.float32
            ) * (LOG2E / math.sqrt(HD))
            before = high[:, span]
            raised = jnp.maximum(before, jnp.max(scores, axis=0, keepdims=True))
            fade = jnp.exp2(before - raised)
            probs = jnp.exp2(scores - raised)
            high[:, span] = raised
            total[:, span] = total[:, span] * fade + jnp.sum(probs, axis=0, keepdims=True)
            acc[:, span] = acc[:, span] * fade + jnp.dot(
                values_t, probs.astype(jnp.bfloat16), preferred_element_type=jnp.float32
            )

    @pl.when(j == NG - 1)
    def _():
        o_ref[...] = (acc[...] / total[...]).T.astype(jnp.bfloat16)


def attend(pattern, place, qh, kv, far):
    grid_spec = pltpu.PrefetchScalarGridSpec(
        num_scalar_prefetch=2,
        grid=(NG,),
        in_specs=[
            pl.BlockSpec((ROWS, HD), lambda j, p, g: (0, 0)),
            pl.BlockSpec((1, 2, ROWS, HD), lambda j, p, g: (jnp.minimum(j, g[0]), 0, 0, 0)),
            pl.BlockSpec((1, 2, ROWS, HD), lambda j, p, g: (jnp.minimum(g[1] + 1, NG - 1), 0, 0, 0)),
            pl.BlockSpec((2, ROWS, HD), lambda j, p, g: (0, 0, 0)),
        ],
        out_specs=[
            pl.BlockSpec((ROWS, HD), lambda j, p, g: (0, 0)),
            pl.BlockSpec((2, ROWS, HD), lambda j, p, g: (0, 0, 0)),
        ],
        scratch_shapes=[
            pltpu.VMEM((HD, ROWS), jnp.float32),
            pltpu.VMEM((1, ROWS), jnp.float32),
            pltpu.VMEM((1, ROWS), jnp.float32),
        ],
    )
    return pl.pallas_call(
        attend_kernel,
        out_shape=(
            jax.ShapeDtypeStruct((ROWS, HD), jnp.bfloat16),
            jax.ShapeDtypeStruct((2, ROWS, HD), jnp.bfloat16),
        ),
        grid_spec=grid_spec,
        name="attend",
    )(pattern, place, qh, kv, kv, far)


def return_kernel(o_ref, hid_ref, gate_ref, fresh_ref, out_ref, landed, send_sem, recv_sem):
    g = lax.axis_index("tm")
    s = lax.axis_index("seq")
    x = s // 8
    p = x % 2
    role = 8 * p + g % 8
    head = 8 * (x - p + g // 8) + s % 8
    barrier = pltpu.get_barrier_semaphore()

    @pl.when(g < NG - 1)
    def _():
        def greet(i, carry):
            h = (s + i) % NS
            xh = h // 8
            above = g + 1
            tm = 8 * (xh % 2) + above % 8
            signal(barrier, tm, 8 * (xh - xh % 2 + above // 8) + h % 8)
            return carry

        lax.fori_loop(0, NS, greet, 0)

    @pl.when(role > 0)
    def _():
        pl.semaphore_wait(barrier, NS)
        cols = pl.ds(pl.multiple_of(head * HD, HD), HD)

        def send(i, carry):
            t = (s + i) % NS
            remote(
                o_ref.at[pl.ds(pl.multiple_of(t * TOK, 8), TOK)],
                landed.at[:, cols],
                send_sem,
                recv_sem,
                role - 1,
                t,
            ).start()
            return carry

        lax.fori_loop(0, NS, send, 0)
        drain(o_ref, send_sem)

    @pl.when(g < NG - 1)
    def _():
        drain(landed, recv_sem)
        out_ref[...] = (
            hid_ref[...].astype(jnp.float32) + gate_ref[...] * landed[...].astype(jnp.float32)
        ).astype(jnp.bfloat16)

    @pl.when(g == NG - 1)
    def _():
        out_ref[...] = fresh_ref[...]


def give_back(o, hid_next, gate_next, fresh):
    vmem = pl.BlockSpec(memory_space=pltpu.VMEM)
    dma = pltpu.SemaphoreType.DMA
    return pl.pallas_call(
        return_kernel,
        out_shape=jax.ShapeDtypeStruct(fresh.shape, jnp.bfloat16),
        in_specs=[vmem] * 4,
        out_specs=vmem,
        scratch_shapes=[pltpu.VMEM(fresh.shape, jnp.bfloat16), dma, dma],
        compiler_params=pltpu.CompilerParams(collective_id=1, has_side_effects=True),
        name="give_back",
    )(o, hid_next, gate_next, fresh)


def body(queries, keys_proj, values, hidden, fresh_latent, gate_table, noise_step, pattern):
    group = lax.axis_index("tm").astype(jnp.int32)
    odd = lax.axis_index("seq").astype(jnp.int32) // 8 % 2
    far = (odd != group // 8) | (group == 7)
    place = jnp.stack([8 * odd + group % 8, group, far.astype(jnp.int32)])
    gate_row = lax.dynamic_slice_in_dim(gate_table, noise_step[0], 1, 0)
    kv, qh, far_cache, hid_next, gate_next = exchange(keys_proj[0], values[0], queries[0], hidden[0], gate_row)
    attended, next_cache = attend(pattern, place, qh, kv, far_cache)
    advanced = give_back(attended, hid_next, gate_next, fresh_latent)
    return (advanced[None], next_cache[None])


def solution(mesh):
    placed = (
        P("tm", "seq", None),
        P("tm", "seq", None),
        P("tm", "seq", None),
        P("tm", "seq", None),
        P("seq", None),
        P(),
        P("tm"),
        P(),
    )
    return jax.shard_map(
        body,
        mesh=mesh,
        in_specs=placed,
        out_specs=(P("tm", "seq", None), P("tm", None, None, "seq")),
        check_vma=False,
    )
```
